768 devices in a mesh: state: 4 (over x), row: 16 (over y, core), col: 12 (over z).
Axes of the slice: x: 4, y: 8, z: 12, core: 2. Of those that a mesh axis runs over, the one named last changes fastest.
Arguments:
- coeff_rows: bfloat16 [8192, 4096], P('row', 'state'), may hold values from -0.09375 to 0.09375
- coeff_cols: bfloat16 [12288, 4096], P('col', 'state'), may hold values from -0.09375 to 0.09375
- occupation: float32 [4096], P('state'), may hold values from 0.05 to 2
- send_list: int32 [4, 16, 12, 16, 2], P('state', 'row', 'col'), may hold values from 0 to 8
- row_phi: bfloat16 [4, 16, 12, 32, 128, 256], P('state', 'row', 'col'), may hold values from -6 to 6
- col_phi: bfloat16 [4, 16, 12, 32, 128, 256], P('state', 'row', 'col'), may hold values from -6 to 6
Outputs:
- density: float32 [4, 16, 12, 256], P('state', 'row', 'col')
The draws below stay inside these ranges and needn't reach their ends.
Inputs may be any that keep to these rules, and one draw needn't show every extreme that they name: `send_list`: a value of 8 relays nothing.
All inputs are finite; a program needn't handle non-finite values.
Results may differ from the reference program's by a relative error of at most 0.004.
Values may be sent and summed in bfloat16 or wider, within the bound.
A program may use at most 32 MiB of HBM per device.

```python
import math
import jax
import jax.numpy as jnp
from jax import lax

NS = 4096
PTS = 256
SLOTS = 2
NR = 8192
NC = 12288
SUB = 128
NSUB = 8
RECV = 32
N_STATE = 4
N_ROW = 16
N_COL = 12


def with_ends(entries, own_key, low, largest):
    dims = entries.shape
    spot = [jax.random.randint(jax.random.fold_in(own_key, axis), (), 0, dims[axis]) for axis in range(len(dims))]
    entries = entries.at[tuple(spot)].set(low)
    longest = dims.index(max(dims))
    spot[longest] = (spot[longest] + 1) % dims[longest]
    return entries.at[tuple(spot)].set(largest)


def block_levels(key, extent, pieces, low, largest):
    def one(dim, blocks):
        heights = jax.random.uniform(jax.random.fold_in(jax.random.fold_in(key, 6), dim), (blocks,), jnp.float32, low / len(pieces), largest / len(pieces))
        return jnp.repeat(jnp.exp(heights), extent[dim] // blocks).reshape((-1,) + (1,) * (len(extent) - dim - 1))

    level = one(*pieces[0])
    for cut in pieces[1:]:
        level = level * one(*cut)
    return level


def bell_draw(stream_key, extent, deviation, reach, pieces=(), kind=jnp.bfloat16):
    gain = block_levels(stream_key, extent, pieces, -0.22, 0.18) if pieces else 1.0
    entries = jax.random.normal(stream_key, extent, jnp.float32) * deviation * gain
    return jnp.minimum(jnp.maximum(entries, -reach), reach).astype(kind)


def setup_inputs(seed: int = 0) -> dict:
    key_of = jax.random.split(jax.random.key(seed), 7)
    return {
        "coeff_rows": bell_draw(key_of[0], (NR, NS), NS ** -0.5, 0.09375, ((0, 16), (1, 4))),
        "coeff_cols": bell_draw(key_of[1], (NC, NS), NS ** -0.5, 0.09375, ((0, 12), (1, 4))),
        "occupation": jnp.clip(jnp.exp(math.log(2.0) - 3.6888794 * jax.random.uniform(key_of[2], (NS,), jnp.float32) ** block_levels(key_of[2], (NS,), ((0, 4),), -0.2, 0.2)), 0.05, 2.0),
        "send_list": with_ends(jax.random.randint(key_of[3], (N_STATE, N_ROW, N_COL, N_ROW, SLOTS), 0, NSUB + 1), jax.random.fold_in(key_of[3], 1), 0, NSUB).astype(jnp.int32),
        "row_phi": bell_draw(key_of[4], (N_STATE, N_ROW, N_COL, RECV, SUB, PTS), 1.0, 6.0, ((0, 4), (1, 16), (2, 12))),
        "col_phi": bell_draw(key_of[5], (N_STATE, N_ROW, N_COL, RECV, SUB, PTS), 1.0, 6.0, ((0, 4), (1, 16), (2, 12))),
    }


def reference(coeff_rows, coeff_cols, occupation, send_list, row_phi, col_phi):
    weighted = (coeff_rows.astype(jnp.float32) * occupation[None, :]).astype(jnp.bfloat16)
    matrix = jnp.dot(weighted, coeff_cols.T, preferred_element_type=jnp.float32).astype(jnp.bfloat16)
    tiles = matrix.reshape(N_ROW, N_STATE, SUB, N_COL, NSUB, SUB).transpose(1, 0, 3, 4, 2, 5)
    blank = jnp.zeros((N_STATE, N_ROW, N_COL, 1, SUB, SUB), jnp.bfloat16)
    tiles = jnp.concatenate([tiles, blank], axis=3)
    sources = jnp.arange(N_ROW, dtype=jnp.int32)

    def owner(index):
        s_idx = index // (N_ROW * N_COL)
        r_idx = (index // N_COL) % N_ROW
        c_idx = index % N_COL
        chosen = tiles[s_idx, :, c_idx]
        picks = send_list[s_idx, :, c_idx, r_idx, :]
        got = chosen[sources[:, None], picks].reshape(RECV, SUB, SUB)
        half = jnp.einsum('tab,tbp->tap', got.astype(jnp.float32), col_phi[s_idx, r_idx, c_idx].astype(jnp.float32))
        return jnp.sum(row_phi[s_idx, r_idx, c_idx].astype(jnp.float32) * half, axis=(0, 1))

    owners = jnp.arange(N_STATE * N_ROW * N_COL, dtype=jnp.int32)
    return lax.map(owner, owners).reshape(N_STATE, N_ROW, N_COL, PTS)
```

```python
import functools

import jax
import jax.numpy as jnp
from jax import lax
from jax.experimental import pallas as pl
from jax.experimental.pallas import tpu as pltpu
from jax.sharding import PartitionSpec as P

MESH = pl.DeviceIdType.MESH
CHUNKS = 4
HEAD = 16
OWN, UP, DOWN, FAR = 0, (0, 1, 2, 3), (0, 4, 5, 6), 7


def kernel(
    side, count, occ_ref, list_ref, rows_hbm, cols_hbm, rphi_hbm, cphi_hbm, out_ref,
    rows_v, cols_v, rphi_v, cphi_v, weighted_v, own_v, next_v,
    stage_s, stage_r, plain_s, plain_r, comb_s, comb_r, *rest,
):
    blocks = [[rest[2 * j], rest[2 * j + 1]] for j in range(8)]
    load_sem, xs, xr, ys, yr, ss, sr = rest[16:]
    n_state, n_row = lax.axis_size("state"), lax.axis_size("row")
    chips = n_row // 2
    s, r = lax.axis_index("state"), lax.axis_index("row")
    y, k = r // 2, r % 2
    x_next, x_prev = lax.rem(s + 1, n_state), lax.rem(s + n_state - 1, n_state)
    up = lax.rem(y + 1, chips) * 2 + k
    down = lax.rem(y + chips - 1, chips) * 2 + k
    sibling = y * 2 + 1 - k
    width = count * side // CHUNKS

    barrier = pltpu.get_barrier_semaphore()
    neighbours = ({"state": x_next}, {"state": x_prev}, {"row": up}, {"row": down}, {"row": sibling})
    for who in neighbours:
        pl.semaphore_signal(barrier, inc=1, device_id=who, device_id_type=MESH)

    loads = [
        pltpu.make_async_copy(rows_hbm, rows_v, load_sem.at[0]),
        *(
            pltpu.make_async_copy(
                cols_hbm.at[pl.ds(q * width, width)], cols_v.at[pl.ds(q * width, width)], load_sem.at[1 + q]
            )
            for q in range(CHUNKS)
        ),
        pltpu.make_async_copy(rphi_hbm, rphi_v, load_sem.at[1 + CHUNKS]),
        pltpu.make_async_copy(cphi_hbm, cphi_v, load_sem.at[2 + CHUNKS]),
    ]
    for load in loads:
        load.start()

    picks = list_ref[0, 0, 0].astype(jnp.float32)
    lane = lax.broadcasted_iota(jnp.int32, (n_row, 128), 1)
    picks = jnp.where(
        lane == 0,
        jnp.broadcast_to(picks[:, 0:1], (n_row, 128)),
        jnp.broadcast_to(picks[:, 1:2], (n_row, 128)),
    )
    blocks[OWN][0][pl.ds(0, HEAD), :] = picks.astype(jnp.bfloat16)

    loads[0].wait()
    for j in range(n_state):
        target = lax.rem(s + j, n_state)
        part = rows_v[pl.ds(pl.multiple_of(target * side, side), side), :].astype(jnp.float32)
        weighted_v[pl.ds(j * side, side), :] = (part * occ_ref[...]).astype(jnp.bfloat16)

    sent = []

    def send(src, dst, send_sem, recv_sem, who):
        copy = pltpu.make_async_remote_copy(
            src_ref=src, dst_ref=dst, send_sem=send_sem, recv_sem=recv_sem, device_id=who, device_id_type=MESH
        )
        copy.start()
        sent.append(copy)

    def arrived(dst, send_sem, recv_sem):
        pltpu.make_async_remote_copy(
            src_ref=dst, dst_ref=dst, send_sem=send_sem, recv_sem=recv_sem,
            device_id={"row": sibling}, device_id_type=MESH,
        ).wait_recv()

    def ways(q):
        return (x_next, x_prev) if q % 2 == 0 else (x_prev, x_next)

    def partials(q):
        loads[1 + q].wait()
        product = lax.dot_general(
            weighted_v[...], cols_v[pl.ds(q * width, width), :], (((1,), (1,)), ((), ())),
            preferred_element_type=jnp.float32,
        )
        own_v[q] = product[:side]
        after, before = product[side : 2 * side], product[3 * side :]
        relayed, plain = (after, before) if q % 2 == 0 else (before, after)
        next_v[q] = relayed
        stage_s[q] = product[2 * side : 3 * side].astype(jnp.bfloat16)
        plain_s[q] = plain.astype(jnp.bfloat16)

    def first_sends(q):
        ahead, back = ways(q)
        send(stage_s.at[q], stage_r.at[q], xs.at[0, q], xr.at[0, q], {"state": ahead})
        send(plain_s.at[q], plain_r.at[q], xs.at[1, q], xr.at[1, q], {"state": back})

    def relay(q):
        ahead, _ = ways(q)
        arrived(stage_r.at[q], xs.at[0, q], xr.at[0, q])
        comb_s[q] = (next_v[q] + stage_r[q].astype(jnp.float32)).astype(jnp.bfloat16)
        send(comb_s.at[q], comb_r.at[q], xs.at[2, q], xr.at[2, q], {"state": ahead})

    def span(q):
        return pl.ds(0, HEAD + width) if q == 0 else pl.ds(HEAD + q * width, width)

    def share(j, q):
        send(blocks[j][0].at[span(q)], blocks[j][1].at[span(q)], ss.at[j, q], sr.at[j, q], {"row": sibling})

    def hop(way, h, q):
        path, who = ((UP, up), (DOWN, down))[way]
        if h == 4 and q % 2 != way:
            return
        src = blocks[path[h - 1]][0].at[span(q)]
        dst = blocks[FAR if h == 4 else path[h]][0].at[span(q)]
        send(src, dst, ys.at[way, h - 1, q], yr.at[way, h - 1, q], {"row": who})

    def finish(q):
        arrived(plain_r.at[q], xs.at[1, q], xr.at[1, q])
        arrived(comb_r.at[q], xs.at[2, q], xr.at[2, q])
        total = own_v[q] + plain_r[q].astype(jnp.float32) + comb_r[q].astype(jnp.float32)
        total = total.astype(jnp.bfloat16)
        for t in range(width // side):
            blocks[OWN][0][pl.ds(HEAD + q * width + t * side, side), :] = total[:, t * side : (t + 1) * side]
        hop(0, 1, q)
        hop(1, 1, q)
        share(OWN, q)

    def forward(h, q):
        for way in (0, 1):
            if h == 4 and q % 2 != way:
                continue
            j = FAR if h == 4 else (UP, DOWN)[way][h]
            arrived(blocks[j][0].at[span(q)], ys.at[way, h - 1, q], yr.at[way, h - 1, q])
            if h < 4:
                hop(way, h + 1, q)
            share(j, q)

    row_of = lax.broadcasted_iota(jnp.int32, (HEAD, 128), 0)
    lane_of = lax.broadcasted_iota(jnp.int32, (1, 128), 1)

    def chip_of(j):
        if j == FAR:
            return lax.rem(y + 4, chips)
        if j in UP:
            return lax.rem(y + chips - UP.index(j), chips)
        return lax.rem(y + DOWN.index(j), chips)

    def contract(j, other, total):
        ref = blocks[j][other]
        source = chip_of(j) * 2 + (1 - k if other else k)
        if other:
            for q in range(CHUNKS):
                arrived(ref.at[span(q)], ss.at[j, q], sr.at[j, q])
        mine = jnp.sum(jnp.where(row_of == r, ref[pl.ds(0, HEAD), :].astype(jnp.float32), 0.0), axis=0, keepdims=True)
        got = [None, None]
        wants = [jnp.sum(jnp.where(lane_of == slot, mine, 0.0), axis=1, keepdims=True) for slot in (0, 1)]
        for t in range(count):
            tile = ref[pl.ds(HEAD + t * side, side), :]
            for slot in (0, 1):
                gate = jnp.where(wants[slot] == float(t), 1.0, 0.0)
                gate = jnp.broadcast_to(gate, (side, side)).astype(jnp.bfloat16)
                term = gate * tile
                got[slot] = term if got[slot] is None else got[slot] + term
        for slot in (0, 1):
            m = source * 2 + slot
            half = jnp.dot(got[slot], cphi_v[0, 0, 0, m], preferred_element_type=jnp.float32)
            weighed = rphi_v[0, 0, 0, m].astype(jnp.float32) * half
            total = total + jnp.sum(weighed.reshape(side // 8, 8, weighed.shape[1]), axis=0)
        return total

    partials(0)
    pl.semaphore_wait(barrier, len(neighbours))
    first_sends(0)
    for q in range(1, CHUNKS):
        partials(q)
        first_sends(q)
    relay(0)
    relay(1)
    finish(0)
    relay(2)
    finish(1)
    forward(1, 0)
    relay(3)
    finish(2)
    forward(1, 1)
    finish(3)
    forward(1, 2)
    forward(1, 3)
    for load in loads[1 + CHUNKS :]:
        load.wait()
    for q in range(CHUNKS):
        forward(2, q)
    total = jnp.zeros((8, out_ref.shape[-1]), jnp.float32)
    for j in (OWN, UP[1], DOWN[1]):
        for other in (0, 1):
            total = contract(j, other, total)
    for q in range(CHUNKS):
        forward(3, q)
    for j in (UP[2], DOWN[2]):
        for other in (0, 1):
            total = contract(j, other, total)
    forward(4, 0)
    forward(4, 1)
    for j in (UP[3], DOWN[3]):
        for other in (0, 1):
            total = contract(j, other, total)
    forward(4, 2)
    forward(4, 3)
    for other in (0, 1):
        total = contract(FAR, other, total)
    out_ref[...] = jnp.sum(total, axis=0, keepdims=True)
    for copy in sent:
        copy.wait_send()


def local(coeff_rows, coeff_cols, occupation, send_list, row_phi, col_phi):
    n_state = lax.axis_size("state")
    rows, depth = coeff_rows.shape
    side = rows // n_state
    count = coeff_cols.shape[0] // side
    width = coeff_cols.shape[0] // CHUNKS
    points = row_phi.shape[-1]
    bf16, f32 = jnp.bfloat16, jnp.float32
    dma = pltpu.SemaphoreType.DMA
    vmem = pl.BlockSpec(memory_space=pltpu.VMEM)
    hbm = pl.BlockSpec(memory_space=pl.ANY)
    density = pl.pallas_call(
        functools.partial(kernel, side, count),
        name="density",
        out_shape=jax.ShapeDtypeStruct((1, points), f32),
        in_specs=[vmem, vmem, hbm, hbm, hbm, hbm],
        out_specs=vmem,
        scratch_shapes=[
            pltpu.VMEM(coeff_rows.shape, bf16),
            pltpu.VMEM(coeff_cols.shape, bf16),
            pltpu.VMEM(row_phi.shape, bf16),
            pltpu.VMEM(col_phi.shape, bf16),
            pltpu.VMEM(coeff_rows.shape, bf16),
            *[pltpu.VMEM((CHUNKS, side, width), f32)] * 2,
            *[pltpu.VMEM((CHUNKS, side, width), bf16)] * 6,
            *[pltpu.VMEM((HEAD + count * side, side), bf16)] * 16,
            dma((3 + CHUNKS,)),
            dma((3, CHUNKS)),
            dma((3, CHUNKS)),
            dma((2, 4, CHUNKS)),
            dma((2, 4, CHUNKS)),
            dma((8, CHUNKS)),
            dma((8, CHUNKS)),
        ],
        compiler_params=pltpu.CompilerParams(
            collective_id=0, has_side_effects=True, vmem_limit_bytes=60 * 1024 * 1024
        ),
    )(occupation.reshape(1, depth), send_list, coeff_rows, coeff_cols, row_phi, col_phi)
    return density.reshape(1, 1, 1, -1)


def solution(mesh):
    in_specs = (
        P("row", "state"),
        P("col", "state"),
        P("state"),
        P("state", "row", "col", None, None),
        P("state", "row", "col", None, None, None),
        P("state", "row", "col", None, None, None),
    )
    out_specs = P("state", "row", "col", None)
    return jax.shard_map(local, mesh=mesh, in_specs=in_specs, out_specs=out_specs, check_vma=False)
```

```python
import functools

import jax
import jax.numpy as jnp
from jax import lax
from jax.experimental import pallas as pl
from jax.experimental.pallas import tpu as pltpu
from jax.sharding import PartitionSpec as P

MESH = pl.DeviceIdType.MESH
HEAD = 16
FIRST = (0, 1, 2, 4, 6, 7)
TILES = (1, 1, 2, 2, 1, 1)
DOTS = ((0, 1), (2,), (3,), (4, 5))
CHUNKS = len(TILES)
OWN, UP, DOWN, FAR = 0, (0, 1, 2, 3), (0, 4, 5, 6), 7


def kernel(
    side, count, occ_ref, list_ref, rows_hbm, cols_hbm, rphi_hbm, cphi_hbm, out_ref,
    rows_v, cols_v, rphi_v, cphi_v, weighted_v, head_v, *rest,
):
    own_v, next_v, stage_s, stage_r, plain_s, plain_r, comb_s, comb_r = (
        rest[i * CHUNKS : (i + 1) * CHUNKS] for i in range(8)
    )
    rest = rest[8 * CHUNKS :]
    blocks = [[rest[2 * j], rest[2 * j + 1]] for j in range(8)]
    load_sem, xs, xr, ys, yr, ss, sr = rest[16:]
    n_state, n_row = lax.axis_size("state"), lax.axis_size("row")
    chips = n_row // 2
    s, r = lax.axis_index("state"), lax.axis_index("row")
    y, k = r // 2, r % 2
    x_next, x_prev = lax.rem(s + 1, n_state), lax.rem(s + n_state - 1, n_state)
    up = lax.rem(y + 1, chips) * 2 + k
    down = lax.rem(y + chips - 1, chips) * 2 + k
    sibling = y * 2 + 1 - k
    width = count * side // len(DOTS)

    barrier = pltpu.get_barrier_semaphore()
    neighbours = ({"state": x_next}, {"state": x_prev}, {"row": up}, {"row": down}, {"row": sibling})
    for who in neighbours:
        pl.semaphore_signal(barrier, inc=1, device_id=who, device_id_type=MESH)

    def local_copy(src, dst, n):
        copy = pltpu.make_async_copy(src, dst, load_sem.at[n])
        copy.start()
        return copy

    row_loads = []
    for j in range(n_state):
        target = pl.multiple_of(lax.rem(s + j, n_state) * side, side)
        row_loads.append(local_copy(rows_hbm.at[pl.ds(target, side)], rows_v.at[pl.ds(j * side, side)], j))
    col_loads = []
    for g in range(len(DOTS)):
        part = pl.ds(g * width, width)
        col_loads.append(local_copy(cols_hbm.at[part], cols_v.at[part], 4 + g))
    phi_loads = [local_copy(rphi_hbm, rphi_v, 8), local_copy(cphi_hbm, cphi_v, 9)]

    head_v[...] = jnp.zeros_like(head_v)
    head_v[pl.ds(0, 2), pl.ds(0, n_row)] = list_ref[0, 0, 0].astype(jnp.float32)
    blocks[OWN][0][pl.ds(0, HEAD), :] = head_v[...].astype(jnp.bfloat16)

    for j in range(n_state):
        row_loads[j].wait()
        part = rows_v[pl.ds(j * side, side), :].astype(jnp.float32)
        weighted_v[pl.ds(j * side, side), :] = (part * occ_ref[...]).astype(jnp.bfloat16)

    sent = []

    def send(src, dst, send_sem, recv_sem, who):
        copy = pltpu.make_async_remote_copy(
            src_ref=src, dst_ref=dst, send_sem=send_sem, recv_sem=recv_sem, device_id=who, device_id_type=MESH
        )
        copy.start()
        sent.append(copy)

    def arrived(dst, send_sem, recv_sem):
        pltpu.make_async_remote_copy(
            src_ref=dst, dst_ref=dst, send_sem=send_sem, recv_sem=recv_sem,
            device_id={"row": sibling}, device_id_type=MESH,
        ).wait_recv()

    def ways(q):
        return (x_next, x_prev) if q % 2 == 0 else (x_prev, x_next)

    def partials(g):
        col_loads[g].wait()
        product = lax.dot_general(
            weighted_v[...], cols_v[pl.ds(g * width, width), :], (((1,), (1,)), ((), ())),
            preferred_element_type=jnp.float32,
        )
        start = 0
        for q in DOTS[g]:
            part = product[:, start : start + TILES[q] * side]
            start += TILES[q] * side
            after, before = part[side : 2 * side], part[3 * side :]
            relayed, plain = (after, before) if q % 2 == 0 else (before, after)
            stage_s[q][...] = part[2 * side : 3 * side].astype(jnp.bfloat16)
            plain_s[q][...] = plain.astype(jnp.bfloat16)
            next_v[q][...] = relayed
            own_v[q][...] = part[:side]

    def first_sends(q):
        ahead, back = ways(q)
        send(stage_s[q], stage_r[q], xs.at[0, q], xr.at[0, q], {"state": ahead})
        send(plain_s[q], plain_r[q], xs.at[1, q], xr.at[1, q], {"state": back})

    def relay(q):
        ahead, _ = ways(q)
        arrived(stage_r[q], xs.at[0, q], xr.at[0, q])
        comb_s[q][...] = (next_v[q][...] + stage_r[q][...].astype(jnp.float32)).astype(jnp.bfloat16)
        send(comb_s[q], comb_r[q], xs.at[2, q], xr.at[2, q], {"state": ahead})

    def span(q):
        if q == 0:
            return pl.ds(0, HEAD + TILES[0] * side)
        return pl.ds(HEAD + FIRST[q] * side, TILES[q] * side)

    def share(j, q):
        send(blocks[j][0].at[span(q)], blocks[j][1].at[span(q)], ss.at[j, q], sr.at[j, q], {"row": sibling})

    def hop(way, h, q):
        path, who = ((UP, up), (DOWN, down))[way]
        if h == 4 and q % 2 != way:
            return
        src = blocks[path[h - 1]][0].at[span(q)]
        dst = blocks[FAR if h == 4 else path[h]][0].at[span(q)]
        send(src, dst, ys.at[way, h - 1, q], yr.at[way, h - 1, q], {"row": who})

    def finish(q):
        arrived(plain_r[q], xs.at[1, q], xr.at[1, q])
        arrived(comb_r[q], xs.at[2, q], xr.at[2, q])
        total = own_v[q][...] + plain_r[q][...].astype(jnp.float32) + comb_r[q][...].astype(jnp.float32)
        total = total.astype(jnp.bfloat16)
        for t in range(TILES[q]):
            blocks[OWN][0][pl.ds(HEAD + (FIRST[q] + t) * side, side), :] = total[:, t * side : (t + 1) * side]
        hop(0, 1, q)
        hop(1, 1, q)
        share(OWN, q)

    def forward(way, h, q):
        j = FAR if h == 4 else (UP, DOWN)[way][h]
        arrived(blocks[j][0].at[span(q)], ys.at[way, h - 1, q], yr.at[way, h - 1, q])
        if h < 4:
            hop(way, h + 1, q)
        share(j, q)

    def forward_both(h, q):
        forward(0, h, q)
        forward(1, h, q)

    lane_of = lax.broadcasted_iota(jnp.int32, (HEAD, 128), 1)

    def chip_of(j):
        if j == FAR:
            return lax.rem(y + 4, chips)
        if j in UP:
            return lax.rem(y + chips - UP.index(j), chips)
        return lax.rem(y + DOWN.index(j), chips)

    def contract(j, other, total):
        ref = blocks[j][other]
        source = chip_of(j) * 2 + (1 - k if other else k)
        if other:
            for q in range(CHUNKS):
                arrived(ref.at[span(q)], ss.at[j, q], sr.at[j, q])
        head = jnp.where(lane_of == r, ref[pl.ds(0, HEAD), :].astype(jnp.float32), 0.0)
        head = jnp.sum(head, axis=1, keepdims=True)
        wants = [head[slot : slot + 1] for slot in (0, 1)]
        got = [None, None]
        for t in range(count):
            tile = ref[pl.ds(HEAD + t * side, side), :]
            for slot in (0, 1):
                gate = jnp.where(wants[slot] == float(t), 1.0, 0.0)
                gate = jnp.broadcast_to(gate, (side, side)).astype(jnp.bfloat16)
                term = gate * tile
                got[slot] = term if got[slot] is None else got[slot] + term
        for slot in (0, 1):
            m = source * 2 + slot
            half = jnp.dot(got[slot], cphi_v[0, 0, 0, m], preferred_element_type=jnp.float32)
            weighed = rphi_v[0, 0, 0, m].astype(jnp.float32) * half
            total = total + jnp.sum(weighed.reshape(side // 8, 8, weighed.shape[1]), axis=0)
        return total

    partials(0)
    pl.semaphore_wait(barrier, len(neighbours))
    first_sends(0)
    first_sends(1)
    partials(1)
    first_sends(2)
    partials(2)
    partials(3)
    relay(0)
    relay(1)
    first_sends(3)
    relay(2)
    first_sends(4)
    first_sends(5)
    finish(0)
    finish(1)
    relay(3)
    finish(2)
    relay(4)
    relay(5)
    forward_both(1, 0)
    forward_both(1, 1)
    finish(3)
    forward_both(1, 2)
    finish(4)
    finish(5)
    for q in (3, 4, 5):
        forward_both(1, q)
    order = ((0, 2, 4, 1, 3, 5), (1, 3, 5, 0, 2, 4))
    for h in (2, 3):
        for i in range(CHUNKS):
            for way in (0, 1):
                forward(way, h, order[way][i])
    for load in phi_loads:
        load.wait()
    total = jnp.zeros((8, out_ref.shape[-1]), jnp.float32)
    for j in (OWN, UP[1], DOWN[1]):
        for other in (0, 1):
            total = contract(j, other, total)
    forward(0, 4, 0)
    forward(1, 4, 1)
    for j in (UP[2], DOWN[2]):
        for other in (0, 1):
            total = contract(j, other, total)
    for q in (2, 3, 4, 5):
        forward(q % 2, 4, q)
    for j in (UP[3], DOWN[3], FAR):
        for other in (0, 1):
            total = contract(j, other, total)
    out_ref[...] = jnp.sum(total, axis=0, keepdims=True)
    for copy in sent:
        copy.wait_send()


def local(coeff_rows, coeff_cols, occupation, send_list, row_phi, col_phi):
    n_state = lax.axis_size("state")
    rows, depth = coeff_rows.shape
    side = rows // n_state
    count = coeff_cols.shape[0] // side
    points = row_phi.shape[-1]
    bf16, f32 = jnp.bfloat16, jnp.float32
    dma = pltpu.SemaphoreType.DMA
    vmem = pl.BlockSpec(memory_space=pltpu.VMEM)
    hbm = pl.BlockSpec(memory_space=pl.ANY)
    density = pl.pallas_call(
        functools.partial(kernel, side, count),
        name="density",
        out_shape=jax.ShapeDtypeStruct((1, points), f32),
        in_specs=[vmem, vmem, hbm, hbm, hbm, hbm],
        out_specs=vmem,
        scratch_shapes=[
            pltpu.VMEM(coeff_rows.shape, bf16),
            pltpu.VMEM(coeff_cols.shape, bf16),
            pltpu.VMEM(row_phi.shape, bf16),
            pltpu.VMEM(col_phi.shape, bf16),
            pltpu.VMEM(coeff_rows.shape, bf16),
            pltpu.VMEM((HEAD, 128), f32),
            *[pltpu.VMEM((side, n * side), kind) for kind in (f32, f32, *[bf16] * 6) for n in TILES],
            *[pltpu.VMEM((HEAD + count * side, side), bf16)] * 16,
            dma((10,)),
            dma((3, CHUNKS)),
            dma((3, CHUNKS)),
            dma((2, 4, CHUNKS)),
            dma((2, 4, CHUNKS)),
            dma((8, CHUNKS)),
            dma((8, CHUNKS)),
        ],
        compiler_params=pltpu.CompilerParams(
            collective_id=0, has_side_effects=True, vmem_limit_bytes=60 * 1024 * 1024
        ),
    )(occupation.reshape(1, depth), jnp.swapaxes(send_list, 3, 4), coeff_rows, coeff_cols, row_phi, col_phi)
    return density.reshape(1, 1, 1, -1)


def solution(mesh):
    in_specs = (
        P("row", "state"),
        P("col", "state"),
        P("state"),
        P("state", "row", "col", None, None),
        P("state", "row", "col", None, None, None),
        P("state", "row", "col", None, None, None),
    )
    out_specs = P("state", "row", "col", None)
    return jax.shard_map(local, mesh=mesh, in_specs=in_specs, out_specs=out_specs, check_vma=False)
```

```python
import functools

import jax
import jax.numpy as jnp
from jax import lax
from jax.experimental import pallas as pl
from jax.experimental.pallas import tpu as pltpu
from jax.sharding import PartitionSpec as P

MESH = pl.DeviceIdType.MESH
HEAD = 16
FIRST = (0, 1, 2, 4, 6, 7)
TILES = (1, 1, 2, 2, 1, 1)
DOTS = ((0, 1), (2,), (3,), (4, 5))
STEPS = (
    ("dot", 0), ("first", 0), ("first", 1), ("dot", 1), ("first", 2), ("dot", 2), ("dot", 3), ("relay", 0),
    ("relay", 1), ("first", 3), ("relay", 2), ("first", 4), ("first", 5), ("fin", 0), ("fin", 1), ("relay", 3),
    ("fin", 2), ("relay", 4), ("relay", 5), ("fwd", 0, 1, 0), ("fwd", 1, 1, 0), ("fwd", 0, 1, 1), ("fwd", 1, 1, 1),
    ("fin", 3), ("fwd", 0, 1, 2), ("fwd", 1, 1, 2), ("fin", 4), ("fin", 5), ("fwd", 0, 1, 3), ("fwd", 1, 1, 3),
    ("fwd", 0, 1, 4), ("fwd", 1, 1, 4), ("fwd", 0, 1, 5), ("fwd", 1, 1, 5), ("fwd", 0, 2, 0), ("fwd", 1, 2, 1),
    ("fwd", 0, 2, 2), ("fwd", 1, 2, 3), ("fwd", 0, 2, 4), ("fwd", 1, 2, 5), ("fwd", 0, 2, 1), ("fwd", 1, 2, 0),
    ("fwd", 0, 2, 3), ("fwd", 1, 2, 2), ("fwd", 0, 2, 5), ("fwd", 1, 2, 4), ("give", 0), ("give", 1), ("give", 4),
    ("fwd", 0, 3, 0), ("fwd", 1, 3, 1), ("fwd", 0, 3, 2), ("fwd", 1, 3, 3), ("fwd", 0, 3, 4), ("fwd", 1, 3, 5),
    ("fwd", 0, 3, 1), ("fwd", 1, 3, 0), ("fwd", 0, 3, 3), ("fwd", 1, 3, 2), ("fwd", 0, 3, 5), ("fwd", 1, 3, 4),
    ("give", 2), ("give", 5), ("give", 3), ("give", 6), ("keep", 0), ("keep", 1), ("keep", 4), ("take", 0),
    ("take", 1), ("take", 4), ("keep", 2), ("keep", 5), ("fwd", 0, 4, 0), ("fwd", 1, 4, 1), ("fwd", 0, 4, 2),
    ("fwd", 1, 4, 3), ("fwd", 0, 4, 4), ("fwd", 1, 4, 5), ("give", 7), ("keep", 3), ("keep", 6), ("keep", 7),
    ("take", 2), ("take", 5), ("take", 3), ("take", 6), ("take", 7),
)
CHUNKS = len(TILES)
OWN, UP, DOWN, FAR = 0, (0, 1, 2, 3), (0, 4, 5, 6), 7


def kernel(
    side, count, occ_hbm, list_hbm, rows_hbm, cols_hbm, rphi_hbm, cphi_hbm, out_ref,
    rows_v, cols_v, rphi_v, cphi_v, weighted_v, head_v, occ_ref, list_ref, *rest,
):
    own_v, next_v, stage_s, stage_r, plain_s, plain_r, comb_s, comb_r = (
        rest[i * CHUNKS : (i + 1) * CHUNKS] for i in range(8)
    )
    rest = rest[8 * CHUNKS :]
    blocks = rest[:8]
    give_s, give_r, load_sem, xs, xr, ys, yr, gs, gr = rest[8:]
    n_state, n_row = lax.axis_size("state"), lax.axis_size("row")
    chips = n_row // 2
    s, r = lax.axis_index("state"), lax.axis_index("row")
    y, k = r // 2, r % 2
    x_next, x_prev = lax.rem(s + 1, n_state), lax.rem(s + n_state - 1, n_state)
    up = lax.rem(y + 1, chips) * 2 + k
    down = lax.rem(y + chips - 1, chips) * 2 + k
    sibling = y * 2 + 1 - k
    width = count * side // len(DOTS)

    barrier = pltpu.get_barrier_semaphore()
    neighbours = ({"state": x_next}, {"state": x_prev}, {"row": up}, {"row": down}, {"row": sibling})
    for who in neighbours:
        pl.semaphore_signal(barrier, inc=1, device_id=who, device_id_type=MESH)

    def local_copy(src, dst, n):
        copy = pltpu.make_async_copy(src, dst, load_sem.at[n])
        copy.start()
        return copy

    occ_load = local_copy(occ_hbm, occ_ref, 10)
    list_load = local_copy(list_hbm, list_ref, 11)
    row_loads = []
    for j in range(n_state):
        target = pl.multiple_of(lax.rem(s + j, n_state) * side, side)
        row_loads.append(local_copy(rows_hbm.at[pl.ds(target, side)], rows_v.at[pl.ds(j * side, side)], j))
    col_loads = []
    for g in range(len(DOTS)):
        part = pl.ds(g * width, width)
        col_loads.append(local_copy(cols_hbm.at[part], cols_v.at[part], 4 + g))

    occ_load.wait()
    for j in range(n_state):
        row_loads[j].wait()
        part = rows_v[pl.ds(j * side, side), :].astype(jnp.float32)
        weighted_v[pl.ds(j * side, side), :] = (part * occ_ref[...]).astype(jnp.bfloat16)

    sent = []

    def send(src, dst, send_sem, recv_sem, who):
        copy = pltpu.make_async_remote_copy(
            src_ref=src, dst_ref=dst, send_sem=send_sem, recv_sem=recv_sem, device_id=who, device_id_type=MESH
        )
        copy.start()
        sent.append(copy)

    def arrived(dst, send_sem, recv_sem):
        pltpu.make_async_remote_copy(
            src_ref=dst, dst_ref=dst, send_sem=send_sem, recv_sem=recv_sem,
            device_id={"row": sibling}, device_id_type=MESH,
        ).wait_recv()

    def ways(q):
        return (x_next, x_prev) if q % 2 == 0 else (x_prev, x_next)

    def partials(g):
        col_loads[g].wait()
        product = lax.dot_general(
            weighted_v[...], cols_v[pl.ds(g * width, width), :], (((1,), (1,)), ((), ())),
            preferred_element_type=jnp.float32,
        )
        start = 0
        for q in DOTS[g]:
            part = product[:, start : start + TILES[q] * side]
            start += TILES[q] * side
            after, before = part[side : 2 * side], part[3 * side :]
            relayed, plain = (after, before) if q % 2 == 0 else (before, after)
            stage_s[q][...] = part[2 * side : 3 * side].astype(jnp.bfloat16)
            plain_s[q][...] = plain.astype(jnp.bfloat16)
            next_v[q][...] = relayed
            own_v[q][...] = part[:side]

    def first_sends(q):
        ahead, back = ways(q)
        send(stage_s[q], stage_r[q], xs.at[0, q], xr.at[0, q], {"state": ahead})
        send(plain_s[q], plain_r[q], xs.at[1, q], xr.at[1, q], {"state": back})

    def relay(q):
        ahead, _ = ways(q)
        arrived(stage_r[q], xs.at[0, q], xr.at[0, q])
        comb_s[q][...] = (next_v[q][...] + stage_r[q][...].astype(jnp.float32)).astype(jnp.bfloat16)
        send(comb_s[q], comb_r[q], xs.at[2, q], xr.at[2, q], {"state": ahead})

    def span(q):
        if q == 0:
            return pl.ds(0, HEAD + TILES[0] * side)
        return pl.ds(HEAD + FIRST[q] * side, TILES[q] * side)

    def hop(way, h, q):
        path, who = ((UP, up), (DOWN, down))[way]
        if h == 4 and q % 2 != way:
            return
        src = blocks[path[h - 1]].at[span(q)]
        dst = blocks[FAR if h == 4 else path[h]].at[span(q)]
        send(src, dst, ys.at[way, h - 1, q], yr.at[way, h - 1, q], {"row": who})

    def finish(q):
        arrived(plain_r[q], xs.at[1, q], xr.at[1, q])
        arrived(comb_r[q], xs.at[2, q], xr.at[2, q])
        total = own_v[q][...]
        total = total + plain_r[q][...].astype(jnp.float32) + comb_r[q][...].astype(jnp.float32)
        total = total.astype(jnp.bfloat16)
        for t in range(TILES[q]):
            blocks[OWN][pl.ds(HEAD + (FIRST[q] + t) * side, side), :] = total[:, t * side : (t + 1) * side]
        hop(0, 1, q)
        hop(1, 1, q)

    def forward(way, h, q):
        j = FAR if h == 4 else (UP, DOWN)[way][h]
        arrived(blocks[j].at[span(q)], ys.at[way, h - 1, q], yr.at[way, h - 1, q])
        if h < 4:
            hop(way, h + 1, q)

    lane_of = lax.broadcasted_iota(jnp.int32, (HEAD, 128), 1)

    def chip_of(j):
        if j == FAR:
            return lax.rem(y + 4, chips)
        if j in UP:
            return lax.rem(y + chips - UP.index(j), chips)
        return lax.rem(y + DOWN.index(j), chips)

    def picked(j, owner):
        ref = blocks[j]
        head = jnp.where(lane_of == owner, ref[pl.ds(0, HEAD), :].astype(jnp.float32), 0.0)
        head = jnp.sum(head, axis=1, keepdims=True)
        got = [None, None]
        for t in range(count):
            tile = ref[pl.ds(HEAD + t * side, side), :]
            for slot in (0, 1):
                gate = jnp.where(head[slot : slot + 1] == float(t), 1.0, 0.0)
                gate = jnp.broadcast_to(gate, (side, side)).astype(jnp.bfloat16)
                term = gate * tile
                got[slot] = term if got[slot] is None else got[slot] + term
        return got

    def contract(source, got):
        while phi_loads:
            phi_loads.pop().wait()
        for slot in (0, 1):
            m = source * 2 + slot
            half = jnp.dot(got[slot], cphi_v[0, 0, 0, m], preferred_element_type=jnp.float32)
            weighed = rphi_v[0, 0, 0, m].astype(jnp.float32) * half
            part = jnp.sum(weighed.reshape(side // 8, 8, weighed.shape[1]), axis=0)
            totals[:] = [totals[0] + part] if totals else [part]

    def give(j):
        for slot, tile in enumerate(picked(j, sibling)):
            give_s[j, slot] = tile
        send(give_s.at[j], give_r.at[j], gs.at[j], gr.at[j], {"row": sibling})

    def keep(j):
        contract(chip_of(j) * 2 + k, picked(j, r))

    def take(j):
        arrived(give_r.at[j], gs.at[j], gr.at[j])
        contract(chip_of(j) * 2 + 1 - k, [give_r[j, slot] for slot in (0, 1)])

    def dot(g):
        partials(g)
        if g == 0:
            pl.semaphore_wait(barrier, len(neighbours))
            list_load.wait()
            head_v[...] = jnp.zeros_like(head_v)
            head_v[pl.ds(0, 2), pl.ds(0, n_row)] = list_ref[0, 0, 0].astype(jnp.float32)
            blocks[OWN][pl.ds(0, HEAD), :] = head_v[...].astype(jnp.bfloat16)
        if g == len(DOTS) - 1:
            phi_loads.append(local_copy(rphi_hbm, rphi_v, 8))
            phi_loads.append(local_copy(cphi_hbm, cphi_v, 9))

    phi_loads, totals = [], []
    act = {"dot": dot, "first": first_sends, "relay": relay, "fin": finish, "fwd": forward}
    act |= {"give": give, "keep": keep, "take": take}
    for step in STEPS:
        act[step[0]](*step[1:])
    out_ref[...] = jnp.sum(totals[0], axis=0, keepdims=True)
    for copy in sent:
        copy.wait_send()


def local(coeff_rows, coeff_cols, occupation, send_list, row_phi, col_phi):
    n_state = lax.axis_size("state")
    rows, depth = coeff_rows.shape
    side = rows // n_state
    count = coeff_cols.shape[0] // side
    points = row_phi.shape[-1]
    bf16, f32 = jnp.bfloat16, jnp.float32
    dma = pltpu.SemaphoreType.DMA
    vmem = pl.BlockSpec(memory_space=pltpu.VMEM)
    hbm = pl.BlockSpec(memory_space=pl.ANY)
    density = pl.pallas_call(
        functools.partial(kernel, side, count),
        name="density",
        out_shape=jax.ShapeDtypeStruct((1, points), f32),
        in_specs=[hbm] * 6,
        out_specs=vmem,
        scratch_shapes=[
            pltpu.VMEM(coeff_rows.shape, bf16),
            pltpu.VMEM(coeff_cols.shape, bf16),
            pltpu.VMEM(row_phi.shape, bf16),
            pltpu.VMEM(col_phi.shape, bf16),
            pltpu.VMEM(coeff_rows.shape, bf16),
            pltpu.VMEM((HEAD, 128), f32),
            pltpu.VMEM((1, depth), f32),
            pltpu.VMEM((1, 1, 1) + send_list.shape[:2:-1], jnp.int32),
            *[pltpu.VMEM((side, n * side), kind) for kind in (f32, f32, *[bf16] * 6) for n in TILES],
            *[pltpu.VMEM((HEAD + count * side, side), bf16)] * 8,
            *[pltpu.VMEM((8, 2, side, side), bf16)] * 2,
            dma((12,)),
            dma((3, CHUNKS)),
            dma((3, CHUNKS)),
            dma((2, 4, CHUNKS)),
            dma((2, 4, CHUNKS)),
            dma((8,)),
            dma((8,)),
        ],
        compiler_params=pltpu.CompilerParams(
            collective_id=0, has_side_effects=True, vmem_limit_bytes=60 * 1024 * 1024
        ),
    )(occupation.reshape(1, depth), jnp.swapaxes(send_list, 3, 4), coeff_rows, coeff_cols, row_phi, col_phi)
    return density.reshape(1, 1, 1, -1)


def solution(mesh):
    in_specs = (
        P("row", "state"),
        P("col", "state"),
        P("state"),
        P("state", "row", "col", None, None),
        P("state", "row", "col", None, None, None),
        P("state", "row", "col", None, None, None),
    )
    out_specs = P("state", "row", "col", None)
    return jax.shard_map(local, mesh=mesh, in_specs=in_specs, out_specs=out_specs, check_vma=False)
```

```python
import functools

import jax
import jax.numpy as jnp
from jax import lax
from jax.experimental import pallas as pl
from jax.experimental.pallas import tpu as pltpu
from jax.sharding import PartitionSpec as P

MESH = pl.DeviceIdType.MESH
HEAD = 16
FIRST = (0, 1, 2, 4, 6, 7)
TILES = (1, 1, 2, 2, 1, 1)
DOTS = ((0, 1), (2,), (3,), (4, 5))
STEPS = (
    ("dot", 0), ("first", 0), ("first", 1), ("dot", 1), ("first", 2), ("dot", 2), ("dot", 3), ("relay", 0),
    ("relay", 1), ("first", 3), ("relay", 2), ("first", 4), ("first", 5), ("fin", 0), ("fin", 1), ("relay", 3),
    ("fin", 2), ("relay", 4), ("relay", 5), ("fwd", 0, 1, 0), ("fwd", 1, 1, 0), ("fwd", 0, 1, 1), ("fwd", 1, 1, 1),
    ("fin", 3), ("fwd", 0, 1, 2), ("fwd", 1, 1, 2), ("fin", 4), ("fin", 5), ("fwd", 0, 1, 3), ("fwd", 1, 1, 3),
    ("fwd", 0, 1, 4), ("fwd", 1, 1, 4), ("fwd", 0, 1, 5), ("fwd", 1, 1, 5), ("fwd", 0, 2, 0), ("fwd", 1, 2, 1),
    ("fwd", 0, 2, 2), ("fwd", 1, 2, 3), ("fwd", 0, 2, 4), ("fwd", 1, 2, 5), ("fwd", 0, 2, 1), ("fwd", 1, 2, 0),
    ("fwd", 0, 2, 3), ("fwd", 1, 2, 2), ("fwd", 0, 2, 5), ("fwd", 1, 2, 4), ("fwd", 0, 3, 0), ("fwd", 1, 3, 1),
    ("fwd", 0, 3, 2), ("fwd", 1, 3, 3), ("give", 0), ("give", 1), ("give", 4), ("keep", 0), ("fwd", 0, 3, 4),
    ("fwd", 1, 3, 5), ("fwd", 0, 3, 1), ("fwd", 1, 3, 0), ("keep", 1), ("keep", 4), ("fwd", 0, 3, 3),
    ("fwd", 1, 3, 2), ("fwd", 0, 3, 5), ("fwd", 1, 3, 4), ("give", 2), ("give", 5), ("give", 3), ("give", 6),
    ("take", 0), ("take", 1), ("take", 4), ("keep", 2), ("keep", 5), ("keep", 3), ("keep", 6), ("take", 2),
    ("take", 5), ("drain", 20), ("fwd", 0, 4, 0), ("fwd", 1, 4, 1), ("fwd", 0, 4, 2), ("fwd", 1, 4, 3),
    ("fwd", 0, 4, 4), ("fwd", 1, 4, 5), ("give", 7), ("keep", 7), ("take", 3), ("take", 6), ("take", 7),
)
CHUNKS = len(TILES)
OWN, UP, DOWN, FAR = 0, (0, 1, 2, 3), (0, 4, 5, 6), 7


def kernel(
    side, count, occ_hbm, list_hbm, rows_hbm, cols_hbm, rphi_hbm, cphi_hbm, out_ref,
    rows_v, cols_v, rphi_v, cphi_v, weighted_v, head_v, occ_ref, list_ref, *rest,
):
    own_v, next_v, stage_s, stage_r, plain_s, plain_r, comb_s, comb_r = (
        rest[i * CHUNKS : (i + 1) * CHUNKS] for i in range(8)
    )
    rest = rest[8 * CHUNKS :]
    blocks = rest[:8]
    give_s, give_r, load_sem, xs, xr, ys, yr, gs, gr = rest[8:]
    n_state, n_row = lax.axis_size("state"), lax.axis_size("row")
    chips = n_row // 2
    s, r = lax.axis_index("state"), lax.axis_index("row")
    y, k = r // 2, r % 2
    x_next, x_prev = lax.rem(s + 1, n_state), lax.rem(s + n_state - 1, n_state)
    up = lax.rem(y + 1, chips) * 2 + k
    down = lax.rem(y + chips - 1, chips) * 2 + k
    sibling = y * 2 + 1 - k
    width = count * side // len(DOTS)

    barrier = pltpu.get_barrier_semaphore()
    neighbours = ({"state": x_next}, {"state": x_prev}, {"row": up}, {"row": down}, {"row": sibling})
    for who in neighbours:
        pl.semaphore_signal(barrier, inc=1, device_id=who, device_id_type=MESH)

    def local_copy(src, dst, n):
        copy = pltpu.make_async_copy(src, dst, load_sem.at[n])
        copy.start()
        return copy

    occ_load = local_copy(occ_hbm, occ_ref, 10)
    list_load = local_copy(list_hbm, list_ref, 11)
    row_loads = []
    for j in range(n_state):
        target = pl.multiple_of(lax.rem(s + j, n_state) * side, side)
        row_loads.append(local_copy(rows_hbm.at[pl.ds(target, side)], rows_v.at[pl.ds(j * side, side)], j))
    col_loads = []
    for g in range(len(DOTS)):
        part = pl.ds(g * width, width)
        col_loads.append(local_copy(cols_hbm.at[part], cols_v.at[part], 4 + g))

    occ_load.wait()
    for j in range(n_state):
        row_loads[j].wait()
        part = rows_v[pl.ds(j * side, side), :].astype(jnp.float32)
        weighted_v[pl.ds(j * side, side), :] = (part * occ_ref[...]).astype(jnp.bfloat16)

    sent = []

    def send(src, dst, send_sem, recv_sem, who):
        copy = pltpu.make_async_remote_copy(
            src_ref=src, dst_ref=dst, send_sem=send_sem, recv_sem=recv_sem, device_id=who, device_id_type=MESH
        )
        copy.start()
        sent.append(copy)

    def arrived(dst, send_sem, recv_sem):
        pltpu.make_async_remote_copy(
            src_ref=dst, dst_ref=dst, send_sem=send_sem, recv_sem=recv_sem,
            device_id={"row": sibling}, device_id_type=MESH,
        ).wait_recv()

    def ways(q):
        return (x_next, x_prev) if q % 2 == 0 else (x_prev, x_next)

    def partials(g):
        col_loads[g].wait()
        product = lax.dot_general(
            weighted_v[...], cols_v[pl.ds(g * width, width), :], (((1,), (1,)), ((), ())),
            preferred_element_type=jnp.float32,
        )
        start = 0
        for q in DOTS[g]:
            part = product[:, start : start + TILES[q] * side]
            start += TILES[q] * side
            after, before = part[side : 2 * side], part[3 * side :]
            relayed, plain = (after, before) if q % 2 == 0 else (before, after)
            stage_s[q][...] = part[2 * side : 3 * side].astype(jnp.bfloat16)
            plain_s[q][...] = plain.astype(jnp.bfloat16)
            next_v[q][...] = relayed
            own_v[q][...] = part[:side]

    def first_sends(q):
        ahead, back = ways(q)
        send(stage_s[q], stage_r[q], xs.at[0, q], xr.at[0, q], {"state": ahead})
        send(plain_s[q], plain_r[q], xs.at[1, q], xr.at[1, q], {"state": back})

    def relay(q):
        ahead, _ = ways(q)
        arrived(stage_r[q], xs.at[0, q], xr.at[0, q])
        comb_s[q][...] = (next_v[q][...] + stage_r[q][...].astype(jnp.float32)).astype(jnp.bfloat16)
        send(comb_s[q], comb_r[q], xs.at[2, q], xr.at[2, q], {"state": ahead})

    def span(q):
        if q == 0:
            return pl.ds(0, HEAD + TILES[0] * side)
        return pl.ds(HEAD + FIRST[q] * side, TILES[q] * side)

    def hop(way, h, q):
        path, who = ((UP, up), (DOWN, down))[way]
        if h == 4 and q % 2 != way:
            return
        src = blocks[path[h - 1]].at[span(q)]
        dst = blocks[FAR if h == 4 else path[h]].at[span(q)]
        send(src, dst, ys.at[way, h - 1, q], yr.at[way, h - 1, q], {"row": who})

    def finish(q):
        arrived(plain_r[q], xs.at[1, q], xr.at[1, q])
        arrived(comb_r[q], xs.at[2, q], xr.at[2, q])
        total = own_v[q][...]
        total = total + plain_r[q][...].astype(jnp.float32) + comb_r[q][...].astype(jnp.float32)
        total = total.astype(jnp.bfloat16)
        for t in range(TILES[q]):
            blocks[OWN][pl.ds(HEAD + (FIRST[q] + t) * side, side), :] = total[:, t * side : (t + 1) * side]
        hop(0, 1, q)
        hop(1, 1, q)

    def forward(way, h, q):
        j = FAR if h == 4 else (UP, DOWN)[way][h]
        arrived(blocks[j].at[span(q)], ys.at[way, h - 1, q], yr.at[way, h - 1, q])
        if h < 4:
            hop(way, h + 1, q)

    lane_of = lax.broadcasted_iota(jnp.int32, (HEAD, 128), 1)

    def chip_of(j):
        if j == FAR:
            return lax.rem(y + 4, chips)
        if j in UP:
            return lax.rem(y + chips - UP.index(j), chips)
        return lax.rem(y + DOWN.index(j), chips)

    def picked(j, owner):
        ref = blocks[j]
        head = jnp.where(lane_of == owner, ref[pl.ds(0, HEAD), :].astype(jnp.float32), 0.0)
        head = jnp.sum(head, axis=1, keepdims=True)
        got = [None, None]
        for t in range(count):
            tile = ref[pl.ds(HEAD + t * side, side), :]
            for slot in (0, 1):
                gate = jnp.where(head[slot : slot + 1] == float(t), 1.0, 0.0)
                gate = jnp.broadcast_to(gate, (side, side)).astype(jnp.bfloat16)
                term = gate * tile
                got[slot] = term if got[slot] is None else got[slot] + term
        return got

    def contract(source, got):
        while phi_loads:
            phi_loads.pop().wait()
        for slot in (0, 1):
            m = source * 2 + slot
            half = jnp.dot(got[slot], cphi_v[0, 0, 0, m], preferred_element_type=jnp.float32)
            weighed = rphi_v[0, 0, 0, m].astype(jnp.float32) * half
            part = jnp.sum(weighed.reshape(side // 8, 8, weighed.shape[1]), axis=0)
            totals[:] = [totals[0] + part] if totals else [part]

    def give(j):
        for slot, tile in enumerate(picked(j, sibling)):
            give_s[j, slot] = tile
        send(give_s.at[j], give_r.at[j], gs.at[j], gr.at[j], {"row": sibling})

    def keep(j):
        contract(chip_of(j) * 2 + k, picked(j, r))

    def take(j):
        arrived(give_r.at[j], gs.at[j], gr.at[j])
        contract(chip_of(j) * 2 + 1 - k, [give_r[j, slot] for slot in (0, 1)])

    def drain(left):
        while len(sent) > left:
            sent.pop(0).wait_send()

    def dot(g):
        partials(g)
        if g == 0:
            pl.semaphore_wait(barrier, len(neighbours))
            list_load.wait()
            head_v[...] = jnp.zeros_like(head_v)
            head_v[pl.ds(0, 2), pl.ds(0, n_row)] = list_ref[0, 0, 0].astype(jnp.float32)
            blocks[OWN][pl.ds(0, HEAD), :] = head_v[...].astype(jnp.bfloat16)
        if g == len(DOTS) - 1:
            phi_loads.append(local_copy(rphi_hbm, rphi_v, 8))
            phi_loads.append(local_copy(cphi_hbm, cphi_v, 9))

    phi_loads, totals = [], []
    act = {"dot": dot, "first": first_sends, "relay": relay, "fin": finish, "fwd": forward}
    act |= {"give": give, "keep": keep, "take": take, "drain": drain}
    for step in STEPS:
        act[step[0]](*step[1:])
    out_ref[...] = jnp.sum(totals[0], axis=0, keepdims=True)
    drain(0)


def local(coeff_rows, coeff_cols, occupation, send_list, row_phi, col_phi):
    n_state = lax.axis_size("state")
    rows, depth = coeff_rows.shape
    side = rows // n_state
    count = coeff_cols.shape[0] // side
    points = row_phi.shape[-1]
    bf16, f32 = jnp.bfloat16, jnp.float32
    dma = pltpu.SemaphoreType.DMA
    vmem = pl.BlockSpec(memory_space=pltpu.VMEM)
    hbm = pl.BlockSpec(memory_space=pl.ANY)
    density = pl.pallas_call(
        functools.partial(kernel, side, count),
        name="density",
        out_shape=jax.ShapeDtypeStruct((1, points), f32),
        in_specs=[hbm] * 6,
        out_specs=vmem,
        scratch_shapes=[
            pltpu.VMEM(coeff_rows.shape, bf16),
            pltpu.VMEM(coeff_cols.shape, bf16),
            pltpu.VMEM(row_phi.shape, bf16),
            pltpu.VMEM(col_phi.shape, bf16),
            pltpu.VMEM(coeff_rows.shape, bf16),
            pltpu.VMEM((HEAD, 128), f32),
            pltpu.VMEM((1, depth), f32),
            pltpu.VMEM((1, 1, 1) + send_list.shape[:2:-1], jnp.int32),
            *[pltpu.VMEM((side, n * side), kind) for kind in (f32, f32, *[bf16] * 6) for n in TILES],
            *[pltpu.VMEM((HEAD + count * side, side), bf16)] * 8,
            *[pltpu.VMEM((8, 2, side, side), bf16)] * 2,
            dma((12,)),
            dma((3, CHUNKS)),
            dma((3, CHUNKS)),
            dma((2, 4, CHUNKS)),
            dma((2, 4, CHUNKS)),
            dma((8,)),
            dma((8,)),
        ],
        compiler_params=pltpu.CompilerParams(
            collective_id=0, has_side_effects=True, vmem_limit_bytes=60 * 1024 * 1024
        ),
    )(occupation.reshape(1, depth), jnp.swapaxes(send_list, 3, 4), coeff_rows, coeff_cols, row_phi, col_phi)
    return density.reshape(1, 1, 1, -1)


def solution(mesh):
    in_specs = (
        P("row", "state"),
        P("col", "state"),
        P("state"),
        P("state", "row", "col", None, None),
        P("state", "row", "col", None, None, None),
        P("state", "row", "col", None, None, None),
    )
    out_specs = P("state", "row", "col", None)
    return jax.shard_map(local, mesh=mesh, in_specs=in_specs, out_specs=out_specs, check_vma=False)
```
